32 devices in a mesh: enc: 4 (over x, core), own: 8 (over z, y).
Axes of the slice: x: 2, y: 2, z: 4, core: 2. Of those that a mesh axis runs over, the one named last changes fastest.
Arguments:
- features: bfloat16 [2048, 768], P(('enc', 'own')), may hold values from -6 to 6
- doc_cluster: int32 [2048], P(('enc', 'own')), may hold values from 0 to 31, as said below
- norm_gain: float32 [768], replicated, may hold values from 0.25 to 1.75
- w_in: bfloat16 [768, 3072], replicated, may hold values from -0.21875 to 0.21875
- b_in: float32 [3072], replicated, may hold values from -3 to 3
- w_out: bfloat16 [3072, 768], replicated, may hold values from -0.109375 to 0.109375
- members: bfloat16 [8, 4096, 768], P('own', 'enc'), may hold values from -6 to 6
- member_cluster: int32 [8, 4096], P('own', 'enc'), may hold values from 0 to 31, as said below
- cluster_range: int32 [32, 2], replicated, may hold values from 0 to 7, as said below
Outputs:
- embeddings: bfloat16 [2048, 768], P(('enc', 'own'))
- maxsim: float32 [2048], P(('enc', 'own'))
The draws below stay inside these ranges and needn't reach their ends.
Inputs may be any that keep to these rules, and one draw needn't show every extreme that they name: `doc_cluster`: document k of a device's 64 belongs to a cluster whose range lies in owner group g = k mod (2), the owners 4 g to 4 g + 3. Of one device's documents at most 32 belong to clusters whose range holds a given owner; on every device some owner gets exactly 32. `cluster_range`: each cluster's range is an aligned run of 1, 2 or 4 owners inside an aligned group of four owners; every such group has a cluster that spans all four. `member_cluster`: A member's cluster has a range that holds the member's owner, and every owner in a cluster's range holds members of it.
All inputs are finite; a program needn't handle non-finite values.
Results may differ from the reference program's by a relative error of at most 0.0047.
Values may be sent and summed in bfloat16 or wider, within the bound.
No kernel may reach another device: no remote copies, remote signals or barrier semaphores. Data moves between devices by JAX's collectives and lax.ppermute only.
A program may use at most 64 MiB of HBM per device.

```python
import math
import jax
import jax.numpy as jnp
from jax import lax

D = 768
HID = 3072
DOC_DEV = 64
CL_OWN = 4
DOCS = 2048
OWNERS = 8
RES_COL = 4096
NCLUST = 32


def span_table(key):
    index = jnp.arange(NCLUST, dtype=jnp.int32)
    power = jax.random.randint(jax.random.fold_in(key, 11), (NCLUST,), 0, 3)
    drawn = jnp.where(power == 0, 1, jnp.where(power == 1, 2, 4))
    span = jnp.where(index % (4 * CL_OWN) == 0, 4, drawn).astype(jnp.int32)
    anchor = index // CL_OWN
    lowest = anchor - anchor % span
    return (lowest.astype(jnp.int32), (lowest + span - 1).astype(jnp.int32))


def draw_cluster_range(key, part):
    lowest, highest = span_table(key)
    return jnp.stack([lowest, highest], axis=1).astype(jnp.int32)


def draw_doc_cluster(key, part):
    lowest, highest = span_table(key)
    quads = OWNERS // 4
    group = 4 * CL_OWN
    blocks = DOCS // DOC_DEV
    position = jnp.arange(DOC_DEV, dtype=jnp.int32)
    quad = position % quads
    chosen = jax.random.randint(jax.random.fold_in(key, 21), (blocks, DOC_DEV), 0, group)
    entries = quad[None, :] * group + chosen
    heated = jax.random.randint(jax.random.fold_in(key, 22), (blocks,), 0, quads)
    spanning = highest - lowest == 3
    offsets = jnp.arange(group, dtype=jnp.int32)
    candidate = quad[:, None] * group + offsets[None, :]
    allowed = spanning[candidate]
    scores = jax.random.randint(jax.random.fold_in(key, 23), (blocks, DOC_DEV, group), 0, 1 << 16) * group + offsets[None, None, :]
    winner = jnp.argmax(jnp.where(allowed[None, :, :], scores, -1), axis=-1).astype(jnp.int32)
    spread_out = quad[None, :] * group + winner
    result = jnp.where(quad[None, :] == heated[:, None], spread_out, entries)
    return result.reshape(DOCS).astype(jnp.int32)


def draw_member_cluster(key, part):
    lowest, highest = span_table(key)
    owner = jnp.arange(OWNERS, dtype=jnp.int32)
    covers = (lowest[None, :] <= owner[:, None]) & (highest[None, :] >= owner[:, None])
    flags = covers.astype(jnp.int32)
    rank = jnp.cumsum(flags, axis=1) - 1
    number = jnp.sum(flags, axis=1)
    slot = jnp.arange(RES_COL, dtype=jnp.int32)
    first = jnp.argmax((covers[:, None, :] & (rank[:, None, :] == slot[None, :, None])).astype(jnp.int32), axis=-1).astype(jnp.int32)
    labels = jnp.arange(NCLUST, dtype=jnp.int32)
    scores = jax.random.randint(jax.random.fold_in(key, 31), (OWNERS, RES_COL, NCLUST), 0, 1 << 16) * NCLUST + labels[None, None, :]
    other = jnp.argmax(jnp.where(covers[:, None, :], scores, -1), axis=-1).astype(jnp.int32)
    chosen = jnp.where(slot[None, :] < number[:, None], first, other)
    shuffle = jax.random.randint(jax.random.fold_in(key, 32), (OWNERS, RES_COL), 0, 1 << 16) * RES_COL + slot[None, :]
    order = jnp.argsort(shuffle, axis=1).astype(jnp.int32)
    return jnp.take_along_axis(chosen, order, axis=1).astype(jnp.int32)


def shard_levels(stream_key, shape, shards, low, high):
    gain, own = 1.0, jax.random.fold_in(stream_key, 6)
    for dim, parts in shards:
        heights = jnp.exp(jax.random.uniform(jax.random.fold_in(own, dim), (parts,), jnp.float32, low / len(shards), high / len(shards)))
        gain = gain * jnp.repeat(heights, shape[dim] // parts).reshape([-1 if axis == dim else 1 for axis in range(len(shape))])
    return gain


def centred(rng, extent, scale, bound, shards=(), kind=jnp.bfloat16):
    loudness = shard_levels(rng, extent, shards, -0.22, 0.18) if shards else 1.0
    entries = jax.random.normal(rng, extent, jnp.float32) * scale * loudness
    return jnp.minimum(jnp.maximum(entries, -bound), bound).astype(kind)


def setup_inputs(seed: int = 0) -> dict:
    key_of = jax.random.split(jax.random.key(seed), 10)
    features = centred(key_of[0], (DOCS, D), 1.0, 6.0, ((0, 32),))
    doc_cluster = draw_doc_cluster(jax.random.fold_in(key_of[9], 71), 0)
    norm_gain = jnp.clip(1.0 + 0.15 * jax.random.normal(key_of[2], (D,), jnp.float32), 0.25, 1.75)
    w_in = centred(key_of[3], (D, HID), D ** -0.5, 0.21875)
    b_in = centred(key_of[4], (HID,), 0.5, 3.0, (), jnp.float32)
    w_out = centred(key_of[5], (HID, D), HID ** -0.5, 0.109375)
    members = centred(key_of[6], (OWNERS, RES_COL, D), 1.0, 6.0, ((0, 8), (1, 4)))
    member_cluster = draw_member_cluster(jax.random.fold_in(key_of[9], 71), 0)
    cluster_range = draw_cluster_range(jax.random.fold_in(key_of[9], 71), 0)
    return {"features": features, "doc_cluster": doc_cluster, "norm_gain": norm_gain, "w_in": w_in, "b_in": b_in, "w_out": w_out, "members": members, "member_cluster": member_cluster, "cluster_range": cluster_range}


lowest_score = -1e+30

def encode_block(rows, norm_gain, w_in, b_in, w_out):
    inputs = rows.astype(jnp.float32)
    center = inputs - lax.optimization_barrier(jnp.mean(inputs, axis=1, keepdims=True))
    spread = lax.optimization_barrier(jnp.mean(center * center, axis=1, keepdims=True))
    normed = (center * lax.rsqrt(spread + 1e-05) * norm_gain).astype(jnp.bfloat16)
    hidden = jax.nn.gelu(jnp.dot(normed, w_in, preferred_element_type=jnp.float32) + b_in, approximate=True).astype(jnp.bfloat16)
    output = inputs + jnp.dot(hidden, w_out, preferred_element_type=jnp.float32)
    return (output * lax.rsqrt(lax.optimization_barrier(jnp.mean(output * output, axis=1, keepdims=True)) + 1e-06)).astype(jnp.bfloat16)

def best_match(rows, labels, lowest, highest, stored, stored_labels, stored_owner):
    count = rows.shape[0]
    total = stored.shape[0]
    width = rows.shape[1]
    row_block = 2048 if count % 2048 == 0 else count
    col_block = 1024 if total % 1024 == 0 else total
    scale = 1.0 / math.sqrt(width)
    stored_blocks = stored.astype(jnp.float32).reshape(total // col_block, col_block, width)
    label_blocks = stored_labels.reshape(total // col_block, col_block)
    owner_blocks = stored_owner.reshape(total // col_block, col_block)

    def one_block(group):
        block, block_labels, block_low, block_high = group
        block = block.astype(jnp.float32)

        def advance(best, pieces):
            stock, stock_labels, stock_owner = pieces
            score = jnp.dot(block, stock.T, precision=lax.Precision.HIGHEST) * scale
            inside = (block_labels[:, None] == stock_labels[None, :]) & (stock_owner[None, :] >= block_low[:, None]) & (stock_owner[None, :] <= block_high[:, None])
            score = jnp.where(inside, score, lowest_score)
            return (jnp.maximum(best, lax.optimization_barrier(jnp.max(score, axis=1))), None)
        start = jnp.full((block.shape[0],), lowest_score, jnp.float32)
        best, unused = lax.scan(advance, start, (stored_blocks, label_blocks, owner_blocks))
        return best
    result = lax.map(one_block, (rows.reshape(count // row_block, row_block, width), labels.reshape(count // row_block, row_block), lowest.reshape(count // row_block, row_block), highest.reshape(count // row_block, row_block)))
    return result.reshape(count)

def reference(features, doc_cluster, norm_gain, w_in, b_in, w_out, members, member_cluster, cluster_range):
    blocks = features.reshape(DOCS // DOC_DEV, DOC_DEV, D)
    embeddings = lax.map(lambda rows: encode_block(rows, norm_gain, w_in, b_in, w_out), blocks).reshape(DOCS, D)
    quads = OWNERS // 4
    per_block = DOC_DEV // quads
    grouped = embeddings.reshape(DOCS // DOC_DEV, per_block, quads, D).transpose(2, 0, 1, 3).reshape(quads, -1, D)
    labels = doc_cluster.reshape(DOCS // DOC_DEV, per_block, quads).transpose(2, 0, 1).reshape(quads, -1)
    lowest = cluster_range[:, 0][labels]
    highest = cluster_range[:, 1][labels]
    stored = members.reshape(quads, 4 * RES_COL, D)
    stored_labels = member_cluster.reshape(quads, 4 * RES_COL)
    owner_ids = jnp.broadcast_to(jnp.arange(OWNERS, dtype=jnp.int32)[:, None], (OWNERS, RES_COL)).reshape(quads, 4 * RES_COL)
    best = lax.map(lambda group: best_match(*group), (grouped, labels, lowest, highest, stored, stored_labels, owner_ids))
    maxsim = best.reshape(quads, DOCS // DOC_DEV, per_block).transpose(1, 2, 0).reshape(DOCS)
    return (embeddings, maxsim)
```

```python
import functools
import math

import jax
import jax.numpy as jnp
from jax import lax
from jax.experimental import pallas as pl
from jax.experimental.pallas import tpu as pltpu
from jax.sharding import PartitionSpec as P

lowest_score = -1e30
quad = 4
lanes = 128
pad_rows = 16


def whole_spec(space=pltpu.VMEM):
    return pl.BlockSpec(memory_space=space)


def encode_kernel(
    groups,
    features,
    labels,
    gain,
    w_in,
    b_in,
    w_out,
    embeddings,
    own_out,
    cross_out,
    normed,
    total,
    columns,
):
    step = pl.program_id(0)
    docs, width = features.shape
    per = docs // groups

    @pl.when(step == 0)
    def _():
        inputs = features[...].astype(jnp.float32)
        center = inputs - jnp.mean(inputs, axis=1, keepdims=True)
        spread = jnp.mean(center * center, axis=1, keepdims=True)
        normed[...] = (center * lax.rsqrt(spread + 1e-05) * gain[...]).astype(jnp.bfloat16)
        total[...] = inputs

    hidden = jax.nn.gelu(
        jnp.dot(normed[...], w_in[...], preferred_element_type=jnp.float32) + b_in[...],
        approximate=True,
    ).astype(jnp.bfloat16)
    total[...] += jnp.dot(hidden, w_out[...], preferred_element_type=jnp.float32)

    @pl.when(step == pl.num_programs(0) - 1)
    def _():
        output = total[...]
        scaled = output * lax.rsqrt(jnp.mean(output * output, axis=1, keepdims=True) + 1e-06)
        embeddings[...] = scaled.astype(jnp.bfloat16)
        group = lax.axis_index("own") // quad
        blocks = width // lanes
        for block in range(blocks):
            columns[block] = scaled[:, block * lanes : (block + 1) * lanes]
        source = lax.broadcasted_iota(jnp.int32, (docs, lanes), 0)
        column = lax.broadcasted_iota(jnp.int32, (docs, lanes), 1)
        label_rows = jnp.broadcast_to(labels[...].astype(jnp.float32), (pad_rows, docs)).astype(
            jnp.bfloat16
        )
        for shift in range(groups):
            residue = lax.rem(group + shift, groups)
            pick = (source == (column % per) * groups + residue).astype(jnp.bfloat16)
            tags = jnp.dot(label_rows, pick, preferred_element_type=jnp.float32).astype(
                jnp.bfloat16
            )
            for block in range(blocks):
                piece = jnp.zeros((per, lanes), jnp.float32)
                for choice in range(groups):
                    piece = jnp.where(
                        residue == choice,
                        columns[block, pl.ds(choice, per, stride=groups), :],
                        piece,
                    )
                piece = piece.astype(jnp.bfloat16)
                if shift == 0:
                    for peer in range(own_out.shape[0]):
                        own_out[peer, 0, pl.ds(block * per, per), :] = piece
                else:
                    cross_out[shift - 1, pl.ds(block * per, per), :] = piece
            if shift == 0:
                for peer in range(own_out.shape[0]):
                    own_out[peer, 0, pl.ds(blocks * per, pad_rows), :] = tags
            else:
                cross_out[shift - 1, pl.ds(blocks * per, pad_rows), :] = tags


def encode(features, doc_cluster, norm_gain, w_in, b_in, w_out, groups, peers):
    docs, width = features.shape
    hidden = w_in.shape[1]
    chunk = 512 if hidden % 512 == 0 else hidden
    per = docs // groups
    rows = width // lanes * per + pad_rows
    return pl.pallas_call(
        functools.partial(encode_kernel, groups),
        grid=(hidden // chunk,),
        in_specs=[
            pl.BlockSpec((docs, width), lambda i: (0, 0)),
            pl.BlockSpec((1, docs), lambda i: (0, 0)),
            pl.BlockSpec((1, width), lambda i: (0, 0)),
            pl.BlockSpec((width, chunk), lambda i: (0, i)),
            pl.BlockSpec((1, chunk), lambda i: (0, i)),
            pl.BlockSpec((chunk, width), lambda i: (i, 0)),
        ],
        out_specs=[
            pl.BlockSpec((docs, width), lambda i: (0, 0)),
            pl.BlockSpec((peers, 1, rows, lanes), lambda i: (0, 0, 0, 0)),
            pl.BlockSpec((groups - 1, rows, lanes), lambda i: (0, 0, 0)),
        ],
        out_shape=[
            jax.ShapeDtypeStruct((docs, width), jnp.bfloat16),
            jax.ShapeDtypeStruct((peers, 1, rows, lanes), jnp.bfloat16),
            jax.ShapeDtypeStruct((groups - 1, rows, lanes), jnp.bfloat16),
        ],
        scratch_shapes=[
            pltpu.VMEM((docs, width), jnp.bfloat16),
            pltpu.VMEM((docs, width), jnp.float32),
            pltpu.VMEM((width // lanes, docs, lanes), jnp.float32),
        ],
        cost_estimate=pl.CostEstimate(
            flops=4 * docs * width * hidden,
            bytes_accessed=4 * width * hidden,
            transcendentals=docs * hidden,
        ),
        compiler_params=pltpu.CompilerParams(vmem_limit_bytes=24 << 20),
        name="encode",
    )(
        features,
        doc_cluster.reshape(1, docs),
        norm_gain.reshape(1, width),
        pltpu.with_memory_space_constraint(w_in, pltpu.HBM),
        b_in.reshape(1, hidden),
        pltpu.with_memory_space_constraint(w_out, pltpu.HBM),
    )


def tags_kernel(ranges, mine, theirs, out):
    owner = lax.axis_index("own")
    clusters = ranges.shape[0]
    row = 0
    for labels in (mine, theirs):
        value = labels[...]
        inside = jnp.zeros(value.shape, jnp.bool_)
        for cluster in range(clusters):
            held = (ranges[cluster, 0] <= owner) & (owner <= ranges[cluster, 1])
            inside = inside | (value == jnp.where(held, cluster, -2))
        value = jnp.where(inside, value, -1).astype(jnp.float32)
        for line in range(value.shape[0]):
            tall = jnp.broadcast_to(value[line : line + 1, :], (lanes, lanes)).T
            out[pl.ds(row, lanes), :] = tall
            row += lanes


def member_tags(cluster_range, mine, theirs):
    total = mine.size
    return pl.pallas_call(
        tags_kernel,
        in_specs=[whole_spec(pltpu.SMEM), whole_spec(), whole_spec()],
        out_specs=whole_spec(),
        out_shape=jax.ShapeDtypeStruct((2 * total, lanes), jnp.float32),
        cost_estimate=pl.CostEstimate(
            flops=total * lanes, bytes_accessed=8 * total * lanes, transcendentals=0
        ),
        compiler_params=pltpu.CompilerParams(vmem_limit_bytes=4 << 20),
        name="tags",
    )(cluster_range, mine.reshape(-1, lanes), theirs.reshape(-1, lanes))


def best_rows(payload, tags, stores, width):
    peers, slots, rows, unused = payload.shape
    blocks = width // lanes
    per = (rows - pad_rows) // blocks
    count = peers * slots * per
    docs = jnp.concatenate(
        [
            payload[:, :, pl.ds(block * per, per), :].reshape(count, lanes)
            for block in range(blocks)
        ],
        axis=1,
    )
    column = lax.broadcasted_iota(jnp.int32, (1, lanes), 1) // per
    wanted = []
    for start in range(0, count, lanes):
        row = jnp.zeros((1, lanes), jnp.float32)
        for part in range(lanes // per):
            peer, slot = divmod(start // per + part, slots)
            row = jnp.where(
                column == part,
                payload[peer, slot, pl.ds(blocks * per, pad_rows), :][0:1].astype(jnp.float32),
                row,
            )
        wanted.append(row)
    best = [jnp.full((8, lanes), lowest_score, jnp.float32) for unused in wanted]
    tall = 256
    first = 0
    for store in stores:
        for start in range(0, store.shape[0], tall):
            score = lax.dot_general(
                store[pl.ds(start, tall), :],
                docs,
                (((1,), (1,)), ((), ())),
                preferred_element_type=jnp.float32,
            )
            held = tags[pl.ds(first, tall), :]
            first += tall
            for index, row in enumerate(wanted):
                piece = jnp.where(
                    held == row, score[:, index * lanes : (index + 1) * lanes], lowest_score
                )
                best[index] = jnp.maximum(
                    best[index], jnp.max(piece.reshape(tall // 8, 8, lanes), axis=0)
                )
    return [jnp.max(piece, axis=0, keepdims=True) for piece in best]


def own_kernel(payload, tags, mine, theirs, out):
    for index, row in enumerate(best_rows(payload, tags, (mine, theirs), mine.shape[1])):
        out[pl.ds(index, 1), :] = row


def cross_kernel(groups, owners, payload, tags, mine, theirs, own_best, out):
    slots = groups - 1
    peers = payload.shape[0]
    blocks = mine.shape[1] // lanes
    per = (payload.shape[2] - pad_rows) // blocks
    found = best_rows(payload, tags, (mine, theirs), mine.shape[1])
    core = lax.rem(lax.axis_index("enc"), 2)
    group = lax.axis_index("own") // quad
    out[...] = jnp.zeros(out.shape, out.dtype)
    for peer in range(peers):
        across, lane_owner = divmod(peer, quad)
        for shift in range(groups):
            home = lax.rem(group + groups - shift, groups)
            target = (2 * across + core) * owners + home * quad + lane_owner
            if shift == 0:
                row = own_best[pl.ds(peer * per // lanes, 1), :]
            else:
                row = found[(peer * slots + shift - 1) * per // lanes]
            out[target] = row


def finish_kernel(groups, owners, per, scale, received, out):
    slots = groups - 1
    docs = out.shape[1]
    peers = received.shape[0] // (2 * groups)
    encoder = lax.axis_index("enc")
    owner = lax.axis_index("own")
    core = lax.rem(encoder, 2)
    group = owner // quad
    place = (encoder // 2) * quad + lax.rem(owner, quad)
    column = lax.broadcasted_iota(jnp.int32, (8, lanes), 1)
    result = jnp.zeros((8, lanes), jnp.float32)
    for source in range(groups):
        best = jnp.full((1, lanes), lowest_score, jnp.float32)
        for peer in range(peers):
            across, lane_owner = divmod(peer, quad)
            best = jnp.maximum(
                best, received[(2 * across + core) * owners + source * quad + lane_owner]
            )
        shift = lax.rem(source + groups - group, groups)
        position = jnp.where(shift == 0, place, place * slots + shift - 1) * per
        offset = lax.rem(position, lanes)
        index = lax.rem(offset + column // groups, lanes)
        taken = jnp.take_along_axis(jnp.broadcast_to(best, (8, lanes)), index, axis=1)
        result = jnp.where(column % groups == source, taken, result)
    out[...] = (result * scale)[0:1, 0:docs]


def shards(
    features, doc_cluster, norm_gain, w_in, b_in, w_out, members, member_cluster, cluster_range
):
    owners = lax.axis_size("own")
    encoders = lax.axis_size("enc")
    docs, width = features.shape
    groups = owners // quad
    per = docs // groups
    peers = encoders // 2 * quad
    axes = ("enc", "own")
    swap = [(index, index ^ 1) for index in range(encoders)]
    mine = members.reshape(-1, width)
    theirs = lax.ppermute(mine, "enc", swap)
    their_labels = lax.ppermute(member_cluster, "enc", swap)
    embeddings, own_rows, cross_rows = encode(
        features, doc_cluster, norm_gain, w_in, b_in, w_out, groups, peers
    )
    arrived = [
        lax.ppermute(
            cross_rows[shift - 1],
            "own",
            [(index, (index + quad * shift) % owners) for index in range(owners)],
        )
        for shift in range(1, groups)
    ]
    circles = [
        [
            (2 * across + core) * owners + group * quad + lane_owner
            for across in range(encoders // 2)
            for lane_owner in range(quad)
        ]
        for core in range(2)
        for group in range(groups)
    ]
    spread = functools.partial(
        lax.all_to_all,
        axis_name=axes,
        split_axis=0,
        concat_axis=0,
        axis_index_groups=circles,
        tiled=True,
    )
    own_all = spread(own_rows)
    stacked = jnp.stack(arrived)
    cross_all = spread(jnp.broadcast_to(stacked[None], (peers,) + stacked.shape))
    tags = member_tags(cluster_range, member_cluster, their_labels)
    count = peers * per
    cost = pl.CostEstimate(
        flops=4 * count * mine.shape[0] * width,
        bytes_accessed=4 * mine.shape[0] * width,
        transcendentals=0,
    )
    params = pltpu.CompilerParams(vmem_limit_bytes=24 << 20)
    own_best = pl.pallas_call(
        own_kernel,
        in_specs=[whole_spec()] * 4,
        out_specs=whole_spec(),
        out_shape=jax.ShapeDtypeStruct((count // lanes, lanes), jnp.float32),
        cost_estimate=cost,
        compiler_params=params,
        name="own_match",
    )(own_all, tags, mine, theirs)
    replies = pl.pallas_call(
        functools.partial(cross_kernel, groups, owners),
        in_specs=[whole_spec()] * 5,
        out_specs=whole_spec(),
        out_shape=jax.ShapeDtypeStruct((encoders * owners, 1, lanes), jnp.float32),
        cost_estimate=cost,
        compiler_params=params,
        name="cross_match",
    )(cross_all, tags, mine, theirs, own_best)
    received = lax.all_to_all(replies, axes, split_axis=0, concat_axis=0, tiled=True)
    maxsim = pl.pallas_call(
        functools.partial(finish_kernel, groups, owners, per, 1.0 / math.sqrt(width)),
        in_specs=[whole_spec()],
        out_specs=whole_spec(),
        out_shape=jax.ShapeDtypeStruct((1, docs), jnp.float32),
        name="finish",
    )(received)
    return (embeddings, maxsim.reshape(docs))


def solution(mesh):
    placed = (
        P(("enc", "own"), None),
        P(("enc", "own")),
        P(),
        P(),
        P(),
        P(),
        P("own", "enc", None),
        P("own", "enc"),
        P(),
    )
    return jax.shard_map(
        shards,
        mesh=mesh,
        in_specs=placed,
        out_specs=(P(("enc", "own"), None), P(("enc", "own"))),
        check_vma=False,
    )
```

```python
import functools
import math

import jax
import jax.numpy as jnp
from jax import lax
from jax.experimental import pallas as pl
from jax.experimental.pallas import tpu as pltpu
from jax.sharding import PartitionSpec as P

lowest_score = -1e30
quad = 4
lanes = 128
pad_rows = 16


def whole_spec(space=pltpu.VMEM):
    return pl.BlockSpec(memory_space=space)


def from_hbm(value):
    return pltpu.with_memory_space_constraint(value, pltpu.HBM)


def flat(value):
    return len(value.shape) == 1


def stage_kernel(*refs):
    count = (len(refs) - 1) // 2
    sems = refs[-1]
    copies = [
        pltpu.make_async_copy(refs[index], refs[count + index].at[0] if flat(refs[index]) else refs[count + index], sems.at[index])
        for index in range(count)
    ]
    for copy in copies:
        copy.start()
    for copy in copies:
        copy.wait()


def stage(*values):
    return pl.pallas_call(
        stage_kernel,
        in_specs=[whole_spec(pl.ANY)] * len(values),
        out_specs=[whole_spec()] * len(values),
        out_shape=[
            jax.ShapeDtypeStruct((1,) * flat(value) + value.shape, value.dtype) for value in values
        ],
        scratch_shapes=[pltpu.SemaphoreType.DMA((len(values),))],
        cost_estimate=pl.CostEstimate(
            flops=0,
            bytes_accessed=2 * sum(value.size * value.dtype.itemsize for value in values),
            transcendentals=0,
        ),
        compiler_params=pltpu.CompilerParams(vmem_limit_bytes=16 << 20),
        name="stage",
    )(*[from_hbm(value) for value in values])


def split_kernel(groups, features, labels, out, columns):
    docs, width = features.shape
    per = docs // groups
    blocks = width // lanes
    group = lax.axis_index("own") // quad
    for block in range(blocks):
        columns[block] = features[:, block * lanes : (block + 1) * lanes].astype(jnp.float32)
    rows = jnp.broadcast_to(labels[...].astype(jnp.float32), (pad_rows, docs)).astype(jnp.bfloat16)
    for shift in range(1, groups):
        residue = lax.rem(group + shift, groups)
        for block in range(blocks):
            out[shift - 1, pl.ds(block * per, per), :] = residue_rows(
                columns, block, groups, per, residue
            )
        out[shift - 1, pl.ds(blocks * per, pad_rows), :] = residue_tags(rows, groups, per, residue)


def residue_rows(columns, block, groups, per, residue):
    piece = columns[block, pl.ds(0, per, stride=groups), :]
    for choice in range(1, groups):
        piece = jnp.where(
            residue == choice, columns[block, pl.ds(choice, per, stride=groups), :], piece
        )
    return piece.astype(jnp.bfloat16)


def residue_tags(rows, groups, per, residue):
    docs = rows.shape[1]
    source = lax.broadcasted_iota(jnp.int32, (docs, lanes), 0)
    column = lax.broadcasted_iota(jnp.int32, (docs, lanes), 1)
    pick = (source == (column % per) * groups + residue).astype(jnp.bfloat16)
    return jnp.dot(rows, pick, preferred_element_type=jnp.float32).astype(jnp.bfloat16)


def split(features, labels, groups):
    docs, width = features.shape
    rows = width // lanes * (docs // groups) + pad_rows
    return pl.pallas_call(
        functools.partial(split_kernel, groups),
        in_specs=[whole_spec()] * 2,
        out_specs=whole_spec(),
        out_shape=jax.ShapeDtypeStruct((groups - 1, rows, lanes), jnp.bfloat16),
        scratch_shapes=[pltpu.VMEM((width // lanes, docs, lanes), jnp.float32)],
        compiler_params=pltpu.CompilerParams(vmem_limit_bytes=4 << 20),
        name="split",
    )(from_hbm(features), from_hbm(labels))


def encode_kernel(
    groups,
    features,
    labels,
    arrived,
    gain,
    w_in,
    b_in,
    w_out,
    embeddings,
    payload,
    normed,
    columns,
):
    docs, width = features.shape
    hidden = w_in.shape[1]
    per = docs // groups
    blocks = width // lanes
    chunk = 512 if hidden % 512 == 0 else hidden
    inputs = jnp.concatenate(
        [features[...].astype(jnp.float32)]
        + [
            jnp.concatenate(
                [
                    arrived[slot, pl.ds(block * per, per), :].astype(jnp.float32)
                    for block in range(blocks)
                ],
                axis=1,
            )
            for slot in range(groups - 1)
        ],
        axis=0,
    )
    center = inputs - jnp.mean(inputs, axis=1, keepdims=True)
    spread = jnp.mean(center * center, axis=1, keepdims=True)
    normed[...] = (center * lax.rsqrt(spread + 1e-05) * gain[...]).astype(jnp.bfloat16)
    output = inputs
    waiting = None
    for start in range(0, hidden + chunk, chunk):
        raised = None
        if start < hidden:
            raised = (
                jnp.dot(
                    normed[...], w_in[:, pl.ds(start, chunk)], preferred_element_type=jnp.float32
                )
                + b_in[:, pl.ds(start, chunk)]
            )
        if waiting is not None:
            middle = jax.nn.gelu(waiting, approximate=True).astype(jnp.bfloat16)
            output = output + jnp.dot(
                middle, w_out[pl.ds(start - chunk, chunk), :], preferred_element_type=jnp.float32
            )
        waiting = raised
    scaled = output * lax.rsqrt(jnp.mean(output * output, axis=1, keepdims=True) + 1e-06)
    embeddings[...] = scaled[0:docs].astype(jnp.bfloat16)
    group = lax.axis_index("own") // quad
    tags = residue_tags(
        jnp.broadcast_to(labels[...].astype(jnp.float32), (pad_rows, docs)).astype(jnp.bfloat16),
        groups,
        per,
        group,
    )
    column = lax.broadcasted_iota(jnp.int32, (pad_rows, lanes), 1) % docs // per
    for slot in range(1, groups):
        tags = jnp.where(
            column == slot, arrived[slot - 1, pl.ds(blocks * per, pad_rows), :], tags
        )
    for block in range(blocks):
        columns[block] = scaled[0:docs, block * lanes : (block + 1) * lanes]
        pieces = [residue_rows(columns, block, groups, per, group)] + [
            scaled[
                docs + slot * per : docs + (slot + 1) * per, block * lanes : (block + 1) * lanes
            ].astype(jnp.bfloat16)
            for slot in range(groups - 1)
        ]
        for slot in range(groups):
            payload[pl.ds(block * docs + slot * per, per), :] = pieces[slot]
    payload[pl.ds(blocks * docs, pad_rows), :] = tags


def encode(features, labels, arrived, norm_gain, w_in, b_in, w_out, groups):
    docs, width = features.shape
    hidden = w_in.shape[1]
    per = docs // groups
    total = docs + (groups - 1) * per
    rows = width // lanes * docs + pad_rows
    return pl.pallas_call(
        functools.partial(encode_kernel, groups),
        in_specs=[whole_spec()] * 7,
        out_specs=[whole_spec()] * 2,
        out_shape=[
            jax.ShapeDtypeStruct((docs, width), jnp.bfloat16),
            jax.ShapeDtypeStruct((rows, lanes), jnp.bfloat16),
        ],
        scratch_shapes=[
            pltpu.VMEM((total, width), jnp.bfloat16),
            pltpu.VMEM((width // lanes, docs, lanes), jnp.float32),
        ],
        cost_estimate=pl.CostEstimate(
            flops=4 * total * width * hidden,
            bytes_accessed=4 * width * hidden,
            transcendentals=total * hidden,
        ),
        compiler_params=pltpu.CompilerParams(vmem_limit_bytes=20 << 20),
        name="encode",
    )(
        features,
        labels,
        arrived,
        norm_gain,
        w_in,
        b_in,
        w_out,
    )


def tags_kernel(ranges, mine, theirs, store, out, held_store, sem):
    copy = pltpu.make_async_copy(store, held_store, sem)
    copy.start()
    owner = lax.axis_index("own")
    clusters = ranges.shape[0]
    held = []
    for labels in (mine, theirs):
        value = labels[...]
        inside = jnp.zeros(value.shape, jnp.bool_)
        for cluster in range(clusters):
            spans = (ranges[cluster, 0] <= owner) & (owner <= ranges[cluster, 1])
            inside = inside | (value == jnp.where(spans, cluster, -2))
        held.append(jnp.where(inside, value, -1).astype(jnp.float32))
    flat_tags = jnp.concatenate(held, axis=0)
    lines = flat_tags.shape[0]
    square = jnp.concatenate(
        [flat_tags, jnp.zeros((lanes - lines, lanes), jnp.float32)], axis=0
    ).T
    for line in range(lines):
        out[pl.ds(line * lanes, lanes), :] = jnp.broadcast_to(
            square[:, line : line + 1], (lanes, lanes)
        )
    copy.wait()


def member_tags(cluster_range, mine, theirs, store):
    total = mine.size
    return pl.pallas_call(
        tags_kernel,
        in_specs=[whole_spec(pltpu.SMEM), whole_spec(), whole_spec(), whole_spec(pl.ANY)],
        out_specs=[whole_spec()] * 2,
        out_shape=[
            jax.ShapeDtypeStruct((2 * total, lanes), jnp.float32),
            jax.ShapeDtypeStruct(store.shape, store.dtype),
        ],
        scratch_shapes=[pltpu.SemaphoreType.DMA],
        cost_estimate=pl.CostEstimate(
            flops=total * lanes, bytes_accessed=8 * total * lanes, transcendentals=0
        ),
        compiler_params=pltpu.CompilerParams(vmem_limit_bytes=4 << 20),
        name="tags",
    )(
        cluster_range,
        mine.reshape(-1, lanes),
        theirs.reshape(-1, lanes),
        from_hbm(store),
    )


def partner(place, step, peers):
    if peers & (peers - 1) == 0:
        return place ^ step
    return (place + peers - step) % peers


def back(place, step, peers):
    if peers & (peers - 1) == 0:
        return place ^ step
    return (place + step) % peers


def best_rows(docs, chunks, tags, stores):
    blocks = stores[0].shape[1] // lanes
    pair = lanes // docs
    rows = jnp.concatenate(
        [
            jnp.concatenate([chunk[pl.ds(block * docs, docs), :] for chunk in chunks], axis=0)
            for block in range(blocks)
        ],
        axis=1,
    )
    column = lax.broadcasted_iota(jnp.int32, (1, lanes), 1) // docs
    wanted = []
    for first in range(0, len(chunks), pair):
        row = jnp.zeros((1, lanes), jnp.float32)
        for part in range(pair):
            held = chunks[first + part][pl.ds(blocks * docs, pad_rows), :]
            row = jnp.where(column == part, held[0:1].astype(jnp.float32), row)
        wanted.append(row)
    best = [jnp.full((8, lanes), lowest_score, jnp.float32) for unused in wanted]
    tall = 256
    first = 0
    for store in stores:
        for start in range(0, store.shape[0], tall):
            score = lax.dot_general(
                store[pl.ds(start, tall), :],
                rows,
                (((1,), (1,)), ((), ())),
                preferred_element_type=jnp.float32,
            )
            held = tags[pl.ds(first, tall), :]
            first += tall
            for index, row in enumerate(wanted):
                piece = jnp.where(
                    held == row, score[:, index * lanes : (index + 1) * lanes], lowest_score
                )
                best[index] = jnp.maximum(
                    best[index], jnp.max(piece.reshape(tall // 8, 8, lanes), axis=0)
                )
    return [jnp.max(piece, axis=0, keepdims=True) for piece in best]


def early_kernel(docs, tags, mine, theirs, *refs):
    out = refs[-1]
    for index, row in enumerate(best_rows(docs, refs[:-1], tags, (mine, theirs))):
        out[pl.ds(index, 1), :] = row


def late_kernel(groups, owners, docs, peers, tags, mine, theirs, early, *refs):
    out = refs[-1]
    pair = lanes // docs
    rows = [early[pl.ds(index, 1), :] for index in range(early.shape[0])]
    rows = rows + best_rows(docs, refs[:-1], tags, (mine, theirs))
    encoder = lax.axis_index("enc")
    owner = lax.axis_index("own")
    core = lax.rem(encoder, 2)
    group = owner // quad
    place = encoder // 2 * quad + lax.rem(owner, quad)
    out[...] = jnp.zeros(out.shape, out.dtype)
    for slot, step in enumerate(steps_of(peers)):
        home = partner(place, step, peers)
        for shift in range(groups):
            origin = lax.rem(group + groups - shift, groups)
            target = (2 * (home // quad) + core) * owners + origin * quad + lax.rem(home, quad)
            out[target] = rows[slot // pair]


def steps_of(peers):
    def order(step):
        bits = bin(step).count("1")
        return (bits > 0, bits > 1, -bits, step)

    return sorted(range(peers), key=order)


def finish_kernel(groups, owners, per, scale, received, out):
    docs = out.shape[1]
    peers = received.shape[0] // (2 * groups)
    pair = lanes // docs
    encoder = lax.axis_index("enc")
    owner = lax.axis_index("own")
    core = lax.rem(encoder, 2)
    group = owner // quad
    place = (encoder // 2) * quad + lax.rem(owner, quad)
    column = lax.broadcasted_iota(jnp.int32, (8, lanes), 1)
    result = jnp.full((8, lanes), lowest_score, jnp.float32)
    for source in range(groups):
        shift = lax.rem(source + groups - group, groups)
        for part in range(pair):
            best = jnp.full((1, lanes), lowest_score, jnp.float32)
            for slot, step in enumerate(steps_of(peers)):
                if slot % pair == part:
                    sender = back(place, step, peers)
                    row = (2 * (sender // quad) + core) * owners + source * quad
                    best = jnp.maximum(best, received[row + lax.rem(sender, quad)])
            index = lax.rem(part * docs + shift * per + column // groups, lanes)
            taken = jnp.take_along_axis(jnp.broadcast_to(best, (8, lanes)), index, axis=1)
            result = jnp.where(column % groups == source, jnp.maximum(result, taken), result)
    out[...] = (result * scale)[0:1, 0:docs]


def program(
    features, doc_cluster, norm_gain, w_in, b_in, w_out, members, member_cluster, cluster_range
):
    owners = lax.axis_size("own")
    encoders = lax.axis_size("enc")
    docs, width = features.shape
    groups = owners // quad
    per = docs // groups
    peers = encoders // 2 * quad
    axes = ("enc", "own")
    swap = [(index, index ^ 1) for index in range(encoders)]
    mine = members.reshape(-1, width)
    labels = doc_cluster.reshape(1, docs)
    leaving = split(features, labels, groups)
    arrived = []
    for shift in range(1, groups):
        arrived.append(
            lax.ppermute(
                leaving[shift - 1],
                "own",
                [(index, (index + quad * shift) % owners) for index in range(owners)],
            )
        )
    theirs = lax.ppermute(mine, "enc", swap)
    their_labels = lax.ppermute(member_cluster, "enc", swap)
    staged = stage(
        w_in,
        w_out,
        b_in.reshape(1, -1),
        norm_gain,
        features,
        labels,
    )
    w_in, w_out, b_in, norm_gain, features, labels = staged
    embeddings, payload = encode(
        features, labels, jnp.stack(arrived), norm_gain, w_in, b_in, w_out, groups
    )
    tags, theirs = member_tags(cluster_range, member_cluster, their_labels, theirs)
    chunks = []
    for step in steps_of(peers):
        route = []
        for index in range(encoders * owners):
            encoder, owner = divmod(index, owners)
            place = encoder // 2 * quad + owner % quad
            target = back(place, step, peers)
            route.append(
                (
                    index,
                    (2 * (target // quad) + encoder % 2) * owners
                    + owner // quad * quad
                    + target % quad,
                )
            )
        chunks.append(lax.ppermute(payload, axes, route) if step else payload)
    half = peers // 2
    cost = pl.CostEstimate(
        flops=2 * peers * docs * mine.shape[0] * width,
        bytes_accessed=4 * mine.shape[0] * width,
        transcendentals=0,
    )
    params = pltpu.CompilerParams(vmem_limit_bytes=10 << 20)
    early = pl.pallas_call(
        functools.partial(early_kernel, docs),
        in_specs=[whole_spec()] * (3 + half),
        out_specs=whole_spec(),
        out_shape=jax.ShapeDtypeStruct((half * docs // lanes, lanes), jnp.float32),
        cost_estimate=cost,
        compiler_params=params,
        name="early_match",
    )(tags, mine, theirs, *chunks[:half])
    replies = pl.pallas_call(
        functools.partial(late_kernel, groups, owners, docs, peers),
        in_specs=[whole_spec()] * (4 + peers - half),
        out_specs=whole_spec(),
        out_shape=jax.ShapeDtypeStruct((encoders * owners, 1, lanes), jnp.float32),
        cost_estimate=cost,
        compiler_params=params,
        name="late_match",
    )(tags, mine, theirs, early, *chunks[half:])
    received = lax.all_to_all(replies, axes, split_axis=0, concat_axis=0, tiled=True)
    maxsim = pl.pallas_call(
        functools.partial(finish_kernel, groups, owners, per, 1.0 / math.sqrt(width)),
        in_specs=[whole_spec()],
        out_specs=whole_spec(),
        out_shape=jax.ShapeDtypeStruct((1, docs), jnp.float32),
        name="finish",
    )(received)
    return (embeddings, maxsim.reshape(docs))


def solution(mesh):
    placed = (
        P(("enc", "own"), None),
        P(("enc", "own")),
        P(),
        P(),
        P(),
        P(),
        P("own", "enc", None),
        P("own", "enc"),
        P(),
    )
    return jax.shard_map(
        program,
        mesh=mesh,
        in_specs=placed,
        out_specs=(P(("enc", "own"), None), P(("enc", "own"))),
        check_vma=False,
    )
```
